128 devices in a mesh: clip: 4 (over x), seq: 32 (over y, z, core).
Axes of the slice: x: 4, y: 4, z: 4, core: 2. Of those that a mesh axis runs over, the one named last changes fastest.
Arguments:
- queries: bfloat16 [65536, 1024], P(('clip', 'seq')), parts along dimension 0, may hold values from -50 to 50
- rgb_kv: bfloat16 [8, 16384, 1024], P('clip', 'seq'), parts along dimension 0, may hold values from -16 to 16
- tile_ids: int32 [512, 8], P(('clip', 'seq')), parts along dimension 0, may hold values from 0 to 127, as said below
- tile_count: int32 [512], P(('clip', 'seq')), parts along dimension 0, may hold values from 2 to 8
- out_weight: bfloat16 [1024, 1024], replicated, may hold values from -0.1875 to 0.1875
- out_grad: bfloat16 [65536, 1024], P(('clip', 'seq')), parts along dimension 0, may hold values from -6 to 6
Outputs:
- joined: bfloat16 [65536, 1024], P(('clip', 'seq')), parts along dimension 0
- d_queries: bfloat16 [65536, 1024], P(('clip', 'seq')), parts along dimension 0
- d_kv: bfloat16 [8, 16384, 1024], P('clip', 'seq'), parts along dimension 0
- d_out_weight: float32 [4096, 1024], P(('clip', 'seq')), parts along dimension 0
The draws below stay inside these ranges and needn't reach their ends.
There are 4 independent parts, one for each index of `clip`. The reference program is written for one: setup_inputs(seed, part) draws one part's arguments, and reference() takes and returns one part's arrays. A program takes and returns all parts, laid end to end along the dimension named above; an argument that names none is the same for every part. Nothing has to cross between parts.
Inputs may be any that keep to these rules, and one draw needn't show every extreme that they name: `tile_ids`: the 4 consecutive blocks of one group name, in their live entries, at most one distinct tile among tiles 4 s to 4 s + 3, for every s. The entries of one list name distinct tiles.
All inputs are finite; a program needn't handle non-finite values.
Results may differ from the reference program's by a relative error of at most 0.015.
Values may be sent and summed in bfloat16 or wider, within the bound.
No kernel may reach another device: no remote copies, remote signals or barrier semaphores. Data moves between devices by JAX's collectives and lax.ppermute only.
A program may use at most 192 MiB of HBM per device.

```python
import jax
import jax.numpy as jnp
from jax import lax

D = 1024
HEADS = 16
EB = 128
TILE = 128
KMAX = 8
EBLK_DEV = 4
TILE_DEV = 4
NBLK = 128
TOKENS = 16384
NTILE = 128
RGB_TOK = 16384


def block_tables(key):
    sources = NTILE // TILE_DEV
    key_local, key_order, key_count = jax.random.split(jax.random.fold_in(key, 11), 3)
    local_choice = jax.random.randint(key_local, (sources, sources), 0, TILE_DEV)
    ranking = jax.random.randint(key_order, (NBLK, sources), 0, 1 << 20) * sources + jnp.arange(sources)[None, :]
    chosen_sources = jnp.argsort(ranking, axis=1)[:, :KMAX].astype(jnp.int32)
    owner_group = jnp.arange(NBLK) // EBLK_DEV
    chosen_local = jnp.take_along_axis(local_choice[owner_group], chosen_sources, axis=1)
    tile_table = chosen_sources * TILE_DEV + chosen_local
    counts = jax.random.randint(key_count, (NBLK,), 2, KMAX + 1)
    counts = counts.at[0].set(KMAX).at[1].set(2)
    return (tile_table.astype(jnp.int32), counts.astype(jnp.int32))


def float_fields(key):
    parts_list = jax.random.split(jax.random.fold_in(key, 23), 5)
    query_field = jnp.clip(1.2 * jax.random.normal(parts_list[1], (TOKENS, D)), -6.0, 6.0)
    key_field = jnp.clip(1.2 * jax.random.normal(parts_list[3], (RGB_TOK, D)), -6.0, 6.0)
    value_field = jnp.clip(3.0 * jax.random.normal(parts_list[4], (RGB_TOK, D)), -16.0, 16.0)
    return (query_field, key_field, value_field)


def draw_queries(key, part):
    return float_fields(key)[0].astype(jnp.bfloat16)


def draw_rgb_kv(key, part):
    fields = float_fields(key)
    return jnp.stack([fields[1], fields[2]]).astype(jnp.bfloat16)


def draw_tile_ids(key, part):
    return block_tables(key)[0]


def draw_tile_count(key, part):
    return block_tables(key)[1]


def spiked(drawn, key, source, target, shards_of, factor):
    owner, partner = [(jnp.arange(drawn.shape[dim]) // (drawn.shape[dim] // shards_of)).reshape([-1 if axis == dim else 1 for axis in range(drawn.ndim)]) for dim in (source, target)]
    chosen = jax.random.permutation(key, shards_of)[partner]
    strong = (owner == chosen) | (owner == (partner + shards_of // 2) % shards_of)
    return jnp.where(strong, factor * drawn, drawn)


def levels(stream_key, extent, cuts, smallest, largest):
    def one(axis_at, shards_of):
        draws = jax.random.uniform(jax.random.fold_in(jax.random.fold_in(stream_key, 6), axis_at), (shards_of,), jnp.float32, smallest / len(cuts), largest / len(cuts))
        return jnp.repeat(jnp.exp(draws), extent[axis_at] // shards_of).reshape((-1,) + (1,) * (len(extent) - axis_at - 1))

    gain = one(*cuts[0])
    for cut in cuts[1:]:
        gain = gain * one(*cut)
    return gain


def normal_values(own_key, shape, width, most, shards=(), held_as=jnp.bfloat16):
    drawn = jax.random.normal(own_key, shape, jnp.float32) * width
    if len(shards) > 0:
        drawn = levels(own_key, shape, shards, -0.22, 0.18) * drawn
    return jnp.clip(drawn, min=-most, max=most).astype(held_as)


def noise_with(own_key, shape, spread, most, cuts, heavy, held_as=jnp.bfloat16):
    result = spread * jax.random.normal(own_key, shape, jnp.float32)
    if cuts:
        result = result * levels(own_key, shape, cuts, -0.22, 0.18)
    return jnp.clip(spiked(result, jax.random.fold_in(own_key, 3), *heavy), -most, most).astype(held_as)


def setup_inputs(seed: int = 0, part: int = 0) -> dict:
    seeds = jax.random.split(jax.random.key(seed), 7)
    own_keys = jax.random.split(jax.random.fold_in(seeds[6], part), 7)
    queries = draw_queries(jax.random.fold_in(jax.random.fold_in(seeds[6], part), 71), part)
    rgb_kv = draw_rgb_kv(jax.random.fold_in(jax.random.fold_in(seeds[6], part), 71), part)
    tile_ids = draw_tile_ids(jax.random.fold_in(jax.random.fold_in(seeds[6], part), 71), part)
    tile_count = draw_tile_count(jax.random.fold_in(jax.random.fold_in(seeds[6], part), 71), part)
    out_weight = normal_values(seeds[4], (D, D), D ** -0.5, 0.1875)
    out_grad = noise_with(own_keys[5], (TOKENS, D), 1.0, 6.0, ((0, 32),), (0, 1, 32, 2.75))
    return dict(queries=queries, rgb_kv=rgb_kv, tile_ids=tile_ids, tile_count=tile_count, out_weight=out_weight, out_grad=out_grad)


masked_score = -1.0e30


def rounded(values):
    return lax.optimization_barrier(values.astype(jnp.bfloat16))


def reference(queries, rgb_kv, tile_ids, tile_count, out_weight, out_grad):
    sources = NTILE // TILE_DEV
    head_dim = D // HEADS
    score_scale = head_dim ** -0.5
    tile_rows = rgb_kv.reshape(2, NTILE, TILE, D)
    group_queries = queries.reshape(sources, EBLK_DEV, EB, HEADS, head_dim)
    group_ids = tile_ids.reshape(sources, EBLK_DEV, KMAX)
    group_count = tile_count.reshape(sources, EBLK_DEV)
    group_grad = out_grad.reshape(sources, EBLK_DEV * EB, D)

    def one_group(running, inputs):
        query_heads, id_rows, count_rows, grad_rows = inputs
        query_float = query_heads.astype(jnp.float32)
        usable = jnp.arange(KMAX)[None, :] < count_rows[:, None]
        key_rows = tile_rows[0][id_rows].reshape(EBLK_DEV, KMAX * TILE, HEADS, head_dim).astype(jnp.float32)
        value_rows = tile_rows[1][id_rows].reshape(EBLK_DEV, KMAX * TILE, HEADS, head_dim).astype(jnp.float32)
        key_usable = jnp.repeat(usable, TILE, axis=1)
        logits = jnp.einsum("bqhe,bthe->bhqt", query_float, key_rows) * score_scale
        logits = jnp.where(key_usable[:, None, None, :], logits, masked_score)
        row_max = jnp.max(logits, axis=3, keepdims=True)
        row_sum = jnp.sum(jnp.exp(logits - row_max), axis=3, keepdims=True)
        probability = jnp.exp(logits - row_max) / row_sum
        weights = rounded(probability).astype(jnp.float32)
        attended_full = jnp.einsum("bhqt,bthe->bqhe", weights, value_rows)
        attended = rounded(attended_full).reshape(EBLK_DEV * EB, D)
        joined_out = jnp.dot(attended, out_weight, preferred_element_type=jnp.float32).astype(jnp.bfloat16)
        d_attended = rounded(lax.dot_general(grad_rows, out_weight, (((1,), (1,)), ((), ())), preferred_element_type=jnp.float32))
        d_heads = d_attended.reshape(EBLK_DEV, EB, HEADS, head_dim).astype(jnp.float32)
        delta_rows = jnp.sum(d_heads * attended_full, axis=3).transpose(0, 2, 1)[..., None]
        d_weights = jnp.einsum("bqhe,bthe->bhqt", d_heads, value_rows)
        d_scores = rounded(probability * (d_weights - delta_rows)).astype(jnp.float32)
        d_query = (jnp.einsum("bhqt,bthe->bqhe", d_scores, key_rows) * score_scale).astype(jnp.bfloat16)
        d_keys = jnp.einsum("bhqt,bqhe->bthe", d_scores, query_float) * score_scale
        d_values = jnp.einsum("bhqt,bqhe->bthe", weights, d_heads)
        source = id_rows // TILE_DEV
        within = id_rows % TILE_DEV
        matches = (source[:, :, None] == jnp.arange(sources)[None, None, :]) & usable[:, :, None]
        slot_terms = jnp.stack([d_keys.reshape(EBLK_DEV, KMAX, TILE, D), d_values.reshape(EBLK_DEV, KMAX, TILE, D)])
        slot_sums = jnp.einsum("bks,cbktd->cstd", matches.astype(jnp.float32), slot_terms)
        group_terms = rounded(slot_sums).astype(jnp.float32)
        owner_pick = jnp.any(matches[:, :, :, None] & (within[:, :, None, None] == jnp.arange(TILE_DEV)[None, None, None, :]), axis=(0, 1))
        running = running + jnp.einsum("sl,cstd->csltd", owner_pick.astype(jnp.float32), group_terms)
        return running, (joined_out, d_query.reshape(EBLK_DEV * EB, D), attended)

    start = jnp.zeros((2, sources, TILE_DEV, TILE, D), jnp.float32)
    running, outputs = lax.scan(one_group, start, (group_queries, group_ids, group_count, group_grad))
    joined_all, d_query_all, attended_all = outputs
    attended_all = attended_all.reshape(TOKENS, D)
    d_out_weight = jnp.dot(attended_all.T, out_grad, preferred_element_type=jnp.float32)
    d_kv = running.reshape(2, RGB_TOK, D).astype(jnp.bfloat16)
    return joined_all.reshape(TOKENS, D), d_query_all.reshape(TOKENS, D), d_kv, d_out_weight
```

```python
import functools

import jax
import jax.numpy as jnp
from jax import lax
from jax.experimental import pallas as pl
from jax.experimental.pallas import tpu as pltpu
from jax.sharding import PartitionSpec as P


D = 1024
HEADS = 16
EB = 128
TILE = 128
HEAD_DIM = D // HEADS
SCALE = HEAD_DIM ** -0.5
PAIR = 2 * HEAD_DIM
CHUNKS = 4
COLS = D // CHUNKS
NY, NZ, NCORE = 4, 4, 2
LOCAL = 4
DESTS = 8
masked_score = -1e30
ROWS = [[y * NZ * NCORE + i for i in range(NZ * NCORE)] for y in range(NY)]
COLUMNS = [
    [(y * NZ + z) * NCORE + c for y in range(NY) for c in range(NCORE)] for z in range(NZ)
]


def shift(dy, dz, dc):
    pairs = []
    for y in range(NY):
        for z in range(NZ):
            for c in range(NCORE):
                to = (((y + dy) % NY) * NZ + (z + dz) % NZ) * NCORE + (c ^ dc)
                pairs.append(((y * NZ + z) * NCORE + c, to))
    return pairs


def move(x, dy, dz, dc):
    if dy % NY == 0 and dz % NZ == 0 and dc == 0:
        return x
    return lax.ppermute(x, "seq", shift(dy, dz, dc))


def dot(a, b, ca, cb):
    return lax.dot_general(a, b, (((ca,), (cb,)), ((), ())), preferred_element_type=jnp.float32)


def pack_kernel(index_ref, *refs):
    held, packed, sem = refs[:4], refs[4:12], refs[12]
    copies = []
    for d in range(DESTS):
        for k in range(4):
            copy = pltpu.make_async_copy(
                held[k].at[:, index_ref[d, k]], packed[d].at[:, k], sem.at[d, k]
            )
            copy.start()
            copies.append(copy)
    for copy in copies:
        copy.wait()


def pack(index, held):
    shape = jax.ShapeDtypeStruct((2, 4, TILE, COLS), jnp.bfloat16)
    return pl.pallas_call(
        pack_kernel,
        grid_spec=pltpu.PrefetchScalarGridSpec(
            num_scalar_prefetch=1,
            grid=(1,),
            in_specs=[pl.BlockSpec((2, LOCAL, TILE, COLS), lambda i, index: (0, 0, 0, 0))] * 4,
            out_specs=[pl.BlockSpec(memory_space=pl.ANY)] * DESTS,
            scratch_shapes=[pltpu.SemaphoreType.DMA((DESTS, 4))],
        ),
        out_shape=[shape] * DESTS,
        name="pack",
    )(index, *held)


def merge_kernel(index_ref, *refs):
    parts, sums, acc = refs[:8], refs[8:12], refs[12]
    for k in range(4):
        acc[...] = jnp.zeros_like(acc)
        for d in range(DESTS):
            tile = index_ref[d, k]

            @pl.when(tile >= 0)
            def _():
                acc[tile] += parts[d][0, k].astype(jnp.float32)

        sums[k][0] = acc[...].astype(jnp.bfloat16)


def merge(index, parts):
    block = pl.BlockSpec((1, 4, TILE, COLS), lambda i, index: (i, 0, 0, 0))
    shape = jax.ShapeDtypeStruct((2, 4, TILE, COLS), jnp.bfloat16)
    return pl.pallas_call(
        merge_kernel,
        grid_spec=pltpu.PrefetchScalarGridSpec(
            num_scalar_prefetch=1,
            grid=(2,),
            in_specs=[block] * DESTS,
            out_specs=[block] * 4,
            scratch_shapes=[pltpu.VMEM((LOCAL, TILE, COLS), jnp.float32)],
        ),
        out_shape=[shape] * 4,
        name="merge",
    )(index, *parts)


def attention_kernel(blocks, slot_ref, count_ref, q_ref, do_ref, *refs):
    tiles = refs[:8]
    o_ref, dq_ref = refs[8:10]
    grads = refs[10:18]
    keys, values, d_keys, d_values, query2, d_out2, scores, sums = refs[18:]
    for d in range(DESTS):
        for k in range(4):
            keys[4 * d + k] = tiles[d][0, k]
            values[4 * d + k] = tiles[d][1, k]
    d_keys[...] = jnp.zeros_like(d_keys)
    d_values[...] = jnp.zeros_like(d_values)
    first = lax.broadcasted_iota(jnp.int32, (EB, PAIR), 1) < HEAD_DIM
    zero = jnp.zeros((EB, PAIR), jnp.bfloat16)
    trips = count_ref[0]
    for b in range(blocks):
        rows = slice(b * EB, (b + 1) * EB)
        query = q_ref[rows, :] * jnp.bfloat16(SCALE)
        query2[b, :EB, :] = jnp.where(first, query, zero)
        query2[b, EB:, :] = jnp.where(first, zero, query)
        d_out = do_ref[rows, :]
        d_out2[b, :EB, :] = jnp.where(first, d_out, zero)
        d_out2[b, EB:, :] = jnp.where(first, zero, d_out)
        trips = jnp.maximum(trips, count_ref[b])

    def score_step(j, maxima):
        updated = []
        for b in range(blocks):
            logits = dot(keys[slot_ref[b, j]], query2[b], 1, 1)
            logits = jnp.where(j < count_ref[b], logits, masked_score)
            scores[b, j] = logits
            updated.append(
                jnp.maximum(maxima[b], jnp.max(logits.reshape(TILE // 8, 8, 2 * EB), axis=0))
            )
        return tuple(updated)

    maxima = lax.fori_loop(
        0, trips, score_step, (jnp.full((8, 2 * EB), masked_score, jnp.float32),) * blocks
    )
    row_max = [jnp.max(m, axis=0, keepdims=True) for m in maxima]
    sums[...] = jnp.zeros_like(sums)

    def output_step(j, totals):
        updated = []
        for b in range(blocks):
            weight = jnp.exp(scores[b, j] - row_max[b])
            scores[b, j] = weight
            updated.append(totals[b] + jnp.sum(weight.reshape(TILE // 8, 8, 2 * EB), axis=0))
            sums[b] += dot(values[slot_ref[b, j]], weight.astype(jnp.bfloat16), 0, 0)
        return tuple(updated)

    totals = lax.fori_loop(
        0, trips, output_step, (jnp.zeros((8, 2 * EB), jnp.float32),) * blocks
    )
    inverse = [1.0 / jnp.sum(t, axis=0, keepdims=True) for t in totals]
    delta = []
    for b in range(blocks):
        rows = slice(b * EB, (b + 1) * EB)
        out2 = sums[b] * inverse[b]
        out = jnp.concatenate([out2[:HEAD_DIM, :EB], out2[HEAD_DIM:, EB:]], axis=0)
        product = out * do_ref[rows, :].astype(jnp.float32).T
        delta.append(
            jnp.concatenate(
                [
                    jnp.sum(product[:HEAD_DIM], axis=0, keepdims=True),
                    jnp.sum(product[HEAD_DIM:], axis=0, keepdims=True),
                ],
                axis=1,
            )
        )
        o_ref[rows, :] = out.T.astype(jnp.bfloat16)
    sums[...] = jnp.zeros_like(sums)

    def grad_step(j, carry):
        for b in range(blocks):
            slot = slot_ref[b, j]
            weight = scores[b, j] * inverse[b]
            d_weight = dot(values[slot], d_out2[b], 1, 1)
            d_score = (weight * (d_weight - delta[b])).astype(jnp.bfloat16)
            d_values[slot] += dot(weight.astype(jnp.bfloat16), d_out2[b], 1, 0)
            d_keys[slot] += dot(d_score, query2[b], 1, 0)
            sums[b] += dot(keys[slot], d_score, 0, 0)
        return carry

    lax.fori_loop(0, trips, grad_step, 0)
    for b in range(blocks):
        d_query2 = sums[b]
        d_query = jnp.concatenate(
            [d_query2[:HEAD_DIM, :EB], d_query2[HEAD_DIM:, EB:]], axis=0
        )
        dq_ref[b * EB : (b + 1) * EB, :] = (d_query.T * SCALE).astype(jnp.bfloat16)
    for d in range(DESTS):
        for k in range(4):
            grads[d][0, k] = d_keys[4 * d + k].astype(jnp.bfloat16)
            grads[d][1, k] = d_values[4 * d + k].astype(jnp.bfloat16)


def attention(chunk, slots, counts, queries, d_attended, tiles):
    tokens = queries.shape[0]
    blocks = tokens // EB
    entries = slots.shape[1]
    pairs = COLS // PAIR
    wide = pl.BlockSpec((tokens, PAIR), lambda p, s, c: (0, chunk * pairs + p))
    own = pl.BlockSpec((tokens, PAIR), lambda p, s, c: (0, p))
    tile = pl.BlockSpec((2, 4, TILE, PAIR), lambda p, s, c: (0, 0, 0, p))
    out = jax.ShapeDtypeStruct((tokens, COLS), jnp.bfloat16)
    grad = jax.ShapeDtypeStruct((2, 4, TILE, COLS), jnp.bfloat16)
    work = DESTS * 4
    results = pl.pallas_call(
        functools.partial(attention_kernel, blocks),
        grid_spec=pltpu.PrefetchScalarGridSpec(
            num_scalar_prefetch=2,
            grid=(pairs,),
            in_specs=[wide, wide] + [tile] * DESTS,
            out_specs=[own, own] + [tile] * DESTS,
            scratch_shapes=[
                pltpu.VMEM((work, TILE, PAIR), jnp.bfloat16),
                pltpu.VMEM((work, TILE, PAIR), jnp.bfloat16),
                pltpu.VMEM((work, TILE, PAIR), jnp.float32),
                pltpu.VMEM((work, TILE, PAIR), jnp.float32),
                pltpu.VMEM((blocks, 2 * EB, PAIR), jnp.bfloat16),
                pltpu.VMEM((blocks, 2 * EB, PAIR), jnp.bfloat16),
                pltpu.VMEM((blocks, entries, TILE, 2 * EB), jnp.float32),
                pltpu.VMEM((blocks, PAIR, 2 * EB), jnp.float32),
            ],
        ),
        out_shape=[out, out] + [grad] * DESTS,
        cost_estimate=pl.CostEstimate(
            flops=12 * pairs * blocks * entries * TILE * 2 * EB * PAIR,
            transcendentals=pairs * blocks * entries * TILE * 2 * EB,
            bytes_accessed=4 * work * TILE * COLS * 2,
        ),
        compiler_params=pltpu.CompilerParams(vmem_limit_bytes=56 * 1024 * 1024),
        name="attention",
    )(slots, counts, queries, d_attended, *tiles)
    return results[0], results[1], results[2:]


def local(queries, rgb_kv, tile_ids, tile_count, out_weight, out_grad):
    me = lax.axis_index("seq")
    y, z, c = me // (NZ * NCORE), (me // NCORE) % NZ, me % NCORE
    devices = NY * NZ * NCORE
    own_tiles = rgb_kv.reshape(2, LOCAL, TILE, D)
    source = tile_ids // LOCAL
    within = tile_ids % LOCAL
    usable = jnp.arange(tile_ids.shape[1])[None, :] < tile_count[:, None]
    matches = (source[:, :, None] == jnp.arange(devices)[None, None, :]) & usable[:, :, None]
    wanted = jnp.max(jnp.where(matches, within[:, :, None], -1), axis=(0, 1))
    told = [
        lax.all_to_all(
            operand, "seq", 0, 0, axis_index_groups=groups, tiled=True
        ).reshape(-1, NCORE, 4)
        for operand, groups in (
            (wanted.reshape(NY, NZ * NCORE).T, ROWS),
            (wanted.reshape(NY, NZ, NCORE).transpose(0, 2, 1).reshape(-1, NZ), COLUMNS),
        )
    ]
    source_y, source_z = source // (NZ * NCORE), (source // NCORE) % NZ
    flip = (source % NCORE) ^ c
    back_y, back_z = (y - source_y) % NY, (z - source_z) % NZ
    slots = (
        (back_z * NCORE + flip) * 4 + back_y,
        (back_y * NCORE + flip) * 4 + back_z,
    )
    far = jnp.arange(4)[:, None, None]
    core = c ^ jnp.arange(NCORE)[None, :, None]
    near = jnp.arange(4)[None, None, :]
    asked = (
        told[0][(z + far) % NZ, core, (y - near) % NY].reshape(DESTS, 4),
        told[1][(y + far) % NY, core, (z - near) % NZ].reshape(DESTS, 4),
    )

    d_attended = lax.dot_general(
        out_grad, out_weight, (((1,), (1,)), ((), ())), preferred_element_type=jnp.float32
    ).astype(jnp.bfloat16)

    attended, d_queries, d_kv = [], [], []
    for chunk in range(CHUNKS):
        along_y = chunk % 2 == 0
        kind = 0 if along_y else 1

        def near_move(x, k):
            return move(x, k, 0, 0) if along_y else move(x, 0, k, 0)

        def far_move(x, d, sign):
            step, core = sign * (d // NCORE), d % NCORE
            return move(x, 0, step, core) if along_y else move(x, step, 0, core)

        mine = own_tiles[..., chunk * COLS : (chunk + 1) * COLS]
        held = [near_move(mine, k) for k in range(4)]
        packed = pack(jnp.maximum(asked[kind], 0), held)
        tiles = [far_move(packed[d], d, 1) for d in range(DESTS)]
        out, d_query, grads = attention(chunk, slots[kind], tile_count, queries, d_attended, tiles)
        attended.append(out)
        d_queries.append(d_query)
        parts = [far_move(grads[d], d, -1) for d in range(DESTS)]
        sums = merge(asked[kind], parts)
        returned = [near_move(sums[k], -k) for k in range(4)]
        total = sum(r.astype(jnp.float32) for r in returned)
        d_kv.append(total.astype(jnp.bfloat16))
    attended = jnp.concatenate(attended, axis=1)
    joined = jnp.dot(attended, out_weight, preferred_element_type=jnp.float32).astype(jnp.bfloat16)
    product = lax.dot_general(
        attended, out_grad, (((0,), (0,)), ((), ())), preferred_element_type=jnp.float32
    ).astype(jnp.bfloat16)
    d_out_weight = lax.psum_scatter(
        product, "seq", scatter_dimension=0, tiled=True
    ).astype(jnp.float32)
    d_queries = jnp.concatenate(d_queries, axis=1)
    d_kv = jnp.concatenate(d_kv, axis=3).reshape(rgb_kv.shape)
    return (joined, d_queries, d_kv, d_out_weight)


def solution(mesh):
    placed = (
        P(("clip", "seq"), None),
        P("clip", "seq", None),
        P(("clip", "seq"), None),
        P(("clip", "seq")),
        P(),
        P(("clip", "seq"), None),
    )

    return jax.shard_map(
        local,
        mesh=mesh,
        in_specs=placed,
        out_specs=(
            P(("clip", "seq"), None),
            P(("clip", "seq"), None),
            P("clip", "seq", None),
            P(("clip", "seq"), None),
        ),
        check_vma=False,
    )
```

```python
import functools

import jax
import jax.numpy as jnp
from jax import lax
from jax.experimental import pallas as pl
from jax.experimental.pallas import tpu as pltpu
from jax.sharding import PartitionSpec as P


D = 1024
HEADS = 16
EB = 128
TILE = 128
HEAD_DIM = D // HEADS
SCALE = HEAD_DIM ** -0.5
PAIR = 2 * HEAD_DIM
CHUNKS = 4
COLS = D // CHUNKS
NY, NZ, NCORE = 4, 4, 2
LOCAL = 4
DESTS = 8
masked_score = -1e30
ROWS = [[y * NZ * NCORE + i for i in range(NZ * NCORE)] for y in range(NY)]


def shift(dy, dz, dc):
    pairs = []
    for y in range(NY):
        for z in range(NZ):
            for c in range(NCORE):
                to = (((y + dy) % NY) * NZ + (z + dz) % NZ) * NCORE + (c ^ dc)
                pairs.append(((y * NZ + z) * NCORE + c, to))
    return pairs


def move(x, dy, dz, dc):
    if dy % NY == 0 and dz % NZ == 0 and dc == 0:
        return x
    return lax.ppermute(x, "seq", shift(dy, dz, dc))


def dot(a, b, ca, cb):
    return lax.dot_general(a, b, (((ca,), (cb,)), ((), ())), preferred_element_type=jnp.float32)


def pack_kernel(index_ref, *refs):
    held, packed, sem = refs[:4], refs[4:12], refs[12]
    copies = []
    for d in range(DESTS):
        for k in range(4):
            copy = pltpu.make_async_copy(
                held[k].at[:, index_ref[d, k]], packed[d].at[:, k], sem.at[d, k]
            )
            copy.start()
            copies.append(copy)
    for copy in copies:
        copy.wait()


def pack(index, held):
    shape = jax.ShapeDtypeStruct((2, 4, TILE, COLS), jnp.bfloat16)
    return pl.pallas_call(
        pack_kernel,
        grid_spec=pltpu.PrefetchScalarGridSpec(
            num_scalar_prefetch=1,
            grid=(1,),
            in_specs=[pl.BlockSpec((2, LOCAL, TILE, COLS), lambda i, index: (0, 0, 0, 0))] * 4,
            out_specs=[pl.BlockSpec(memory_space=pl.ANY)] * DESTS,
            scratch_shapes=[pltpu.SemaphoreType.DMA((DESTS, 4))],
        ),
        out_shape=[shape] * DESTS,
        name="pack",
    )(index, *held)


def merge_kernel(index_ref, *refs):
    parts, sums, acc = refs[:8], refs[8:12], refs[12]
    for k in range(4):
        acc[...] = jnp.zeros_like(acc)
        for d in range(DESTS):
            tile = index_ref[d, k]

            @pl.when(tile >= 0)
            def _():
                acc[tile] += parts[d][0, k].astype(jnp.float32)

        sums[k][0] = acc[...].astype(jnp.bfloat16)


def merge(index, parts):
    block = pl.BlockSpec((1, 4, TILE, COLS), lambda i, index: (i, 0, 0, 0))
    shape = jax.ShapeDtypeStruct((2, 4, TILE, COLS), jnp.bfloat16)
    return pl.pallas_call(
        merge_kernel,
        grid_spec=pltpu.PrefetchScalarGridSpec(
            num_scalar_prefetch=1,
            grid=(2,),
            in_specs=[block] * DESTS,
            out_specs=[block] * 4,
            scratch_shapes=[pltpu.VMEM((LOCAL, TILE, COLS), jnp.float32)],
        ),
        out_shape=[shape] * 4,
        name="merge",
    )(index, *parts)


def attention_kernel(blocks, slot_ref, count_ref, q_ref, do_ref, *refs):
    tiles = refs[:8]
    o_ref, dq_ref = refs[8:10]
    grads = refs[10:18]
    keys, values, d_keys, d_values, own_keys, own_values, scores, weights, d_scores = refs[18:]
    entries = slot_ref.shape[1]
    for d in range(DESTS):
        for k in range(4):
            keys[4 * d + k] = tiles[d][0, k]
            values[4 * d + k] = tiles[d][1, k]
    d_keys[...] = jnp.zeros_like(d_keys)
    d_values[...] = jnp.zeros_like(d_values)

    def split(x, axis):
        low = lax.broadcasted_iota(jnp.int32, x.shape, 1 - axis) < HEAD_DIM
        zero = jnp.zeros_like(x)
        return jnp.concatenate([jnp.where(low, x, zero), jnp.where(low, zero, x)], axis=axis)

    def join(x):
        return jnp.concatenate([x[:HEAD_DIM, :EB], x[HEAD_DIM:, EB:]], axis=0)

    def fold(x, op):
        return op(x.reshape(TILE // 8, 8, 2 * EB), axis=0)

    def block_step(b, carry):
        rows = pl.ds(pl.multiple_of(b * EB, EB), EB)
        count = count_ref[b]
        query = q_ref[rows, :] * jnp.bfloat16(SCALE)
        query2 = split(query, 0)
        parts = [slice(j * TILE, (j + 1) * TILE) for j in range(entries)]
        for j in range(entries):
            own_keys[parts[j], :] = keys[slot_ref[b, j]]
            own_values[parts[j], :] = values[slot_ref[b, j]]
        logits = dot(own_keys[...], query2, 1, 1)
        maxima = jnp.full((8, 2 * EB), masked_score, jnp.float32)
        for j in range(entries):
            masked = jnp.where(j < count, logits[parts[j]], masked_score)
            scores[parts[j], :] = masked
            maxima = jnp.maximum(maxima, fold(masked, jnp.max))
        row_max = jnp.max(maxima, axis=0, keepdims=True)
        total = jnp.zeros((8, 2 * EB), jnp.float32)
        for j in range(entries):
            weight = jnp.exp(scores[parts[j], :] - row_max)
            total += fold(weight, jnp.sum)
            weights[parts[j], :] = weight.astype(jnp.bfloat16)
        inverse = 1.0 / jnp.sum(total, axis=0, keepdims=True)
        out = join(dot(own_values[...], weights[...], 0, 0) * inverse)
        d_out = do_ref[rows, :].astype(jnp.float32).T
        product = out * d_out
        delta = jnp.concatenate(
            [
                jnp.sum(product[:HEAD_DIM], axis=0, keepdims=True),
                jnp.sum(product[HEAD_DIM:], axis=0, keepdims=True),
            ],
            axis=1,
        )
        delta = delta * inverse
        o_ref[rows, :] = out.T.astype(jnp.bfloat16)
        low = lax.broadcasted_iota(jnp.int32, (PAIR, EB), 0) < HEAD_DIM
        scaled = d_out * jnp.where(low, inverse[:, :EB], inverse[:, EB:])
        d_out2 = split(scaled.T.astype(jnp.bfloat16), 0)
        d_weights = dot(own_values[...], d_out2, 1, 1)
        for j in range(entries):
            change = (d_weights[parts[j]] - delta).astype(jnp.bfloat16)
            d_scores[parts[j], :] = weights[parts[j], :] * change
        value_terms = dot(weights[...], d_out2, 1, 0)
        key_terms = dot(d_scores[...], query2, 1, 0)
        for j in range(entries):
            d_values[slot_ref[b, j]] += value_terms[parts[j]]
            d_keys[slot_ref[b, j]] += key_terms[parts[j]]
        d_query = join(dot(own_keys[...], d_scores[...], 0, 0))
        dq_ref[rows, :] = (d_query.T * SCALE).astype(jnp.bfloat16)
        return carry

    lax.fori_loop(0, blocks, block_step, 0, unroll=2)
    for d in range(DESTS):
        for k in range(4):
            grads[d][0, k] = d_keys[4 * d + k].astype(jnp.bfloat16)
            grads[d][1, k] = d_values[4 * d + k].astype(jnp.bfloat16)


def attention(chunk, slots, counts, queries, d_attended, tiles):
    tokens = queries.shape[0]
    blocks = tokens // EB
    entries = slots.shape[1]
    pairs = COLS // PAIR
    wide = pl.BlockSpec((tokens, PAIR), lambda p, s, c: (0, chunk * pairs + p))
    own = pl.BlockSpec((tokens, PAIR), lambda p, s, c: (0, p))
    tile = pl.BlockSpec((2, 4, TILE, PAIR), lambda p, s, c: (0, 0, 0, p))
    out = jax.ShapeDtypeStruct((tokens, COLS), jnp.bfloat16)
    grad = jax.ShapeDtypeStruct((2, 4, TILE, COLS), jnp.bfloat16)
    work = DESTS * 4
    results = pl.pallas_call(
        functools.partial(attention_kernel, blocks),
        grid_spec=pltpu.PrefetchScalarGridSpec(
            num_scalar_prefetch=2,
            grid=(pairs,),
            in_specs=[wide, wide] + [tile] * DESTS,
            out_specs=[own, own] + [tile] * DESTS,
            scratch_shapes=[
                pltpu.VMEM((work, TILE, PAIR), jnp.bfloat16),
                pltpu.VMEM((work, TILE, PAIR), jnp.bfloat16),
                pltpu.VMEM((work, TILE, PAIR), jnp.float32),
                pltpu.VMEM((work, TILE, PAIR), jnp.float32),
                pltpu.VMEM((entries * TILE, PAIR), jnp.bfloat16),
                pltpu.VMEM((entries * TILE, PAIR), jnp.bfloat16),
                pltpu.VMEM((entries * TILE, 2 * EB), jnp.float32),
                pltpu.VMEM((entries * TILE, 2 * EB), jnp.bfloat16),
                pltpu.VMEM((entries * TILE, 2 * EB), jnp.bfloat16),
            ],
        ),
        out_shape=[out, out] + [grad] * DESTS,
        cost_estimate=pl.CostEstimate(
            flops=12 * pairs * blocks * entries * TILE * 2 * EB * PAIR,
            transcendentals=pairs * blocks * entries * TILE * 2 * EB,
            bytes_accessed=4 * work * TILE * COLS * 2,
        ),
        compiler_params=pltpu.CompilerParams(vmem_limit_bytes=56 * 1024 * 1024),
        name="attention",
    )(slots, counts, queries, d_attended, *tiles)
    return results[0], results[1], results[2:]


def local(queries, rgb_kv, tile_ids, tile_count, out_weight, out_grad):
    me = lax.axis_index("seq")
    y, z, c = me // (NZ * NCORE), (me // NCORE) % NZ, me % NCORE
    devices = NY * NZ * NCORE
    own_tiles = rgb_kv.reshape(2, LOCAL, TILE, D)
    source = tile_ids // LOCAL
    within = tile_ids % LOCAL
    usable = jnp.arange(tile_ids.shape[1])[None, :] < tile_count[:, None]
    matches = (source[:, :, None] == jnp.arange(devices)[None, None, :]) & usable[:, :, None]
    wanted = jnp.max(jnp.where(matches, within[:, :, None], -1), axis=(0, 1))
    grid = wanted.reshape(NY, NZ, NCORE)
    along = jnp.concatenate(
        [
            jnp.broadcast_to(grid.transpose(1, 2, 0)[None], (NY, NZ, NCORE, NY)),
            jnp.broadcast_to(grid.transpose(0, 2, 1)[:, None], (NY, NZ, NCORE, NZ)),
        ],
        axis=3,
    )
    told = lax.all_to_all(along.reshape(devices, NY + NZ), "seq", 0, 0, tiled=True)
    told = told.reshape(NY, NZ, NCORE, NY + NZ)
    source_y, source_z = source // (NZ * NCORE), (source // NCORE) % NZ
    flip = (source % NCORE) ^ c
    back_y, back_z = (y - source_y) % NY, (z - source_z) % NZ
    slots = (
        (back_z * NCORE + flip) * 4 + back_y,
        (back_y * NCORE + flip) * 4 + back_z,
    )
    far = jnp.arange(4)[:, None, None]
    core = c ^ jnp.arange(NCORE)[None, :, None]
    near = jnp.arange(4)[None, None, :]
    asked = (
        told[y, (z + far) % NZ, core, (y - near) % NY].reshape(DESTS, 4),
        told[(y + far) % NY, z, core, NY + (z - near) % NZ].reshape(DESTS, 4),
    )

    d_attended = lax.dot_general(
        out_grad, out_weight, (((1,), (1,)), ((), ())), preferred_element_type=jnp.float32
    ).astype(jnp.bfloat16)

    attended, d_queries, d_kv, partials = [], [], [], []
    for chunk in range(CHUNKS):
        along_y = chunk % 2 == 0
        kind = 0 if along_y else 1

        def near_move(x, k):
            return move(x, k, 0, 0) if along_y else move(x, 0, k, 0)

        def far_move(x, d, sign):
            step, core = sign * (d // NCORE), d % NCORE
            return move(x, 0, step, core) if along_y else move(x, step, 0, core)

        mine = own_tiles[..., chunk * COLS : (chunk + 1) * COLS]
        held = [near_move(mine, k) for k in range(4)]
        packed = pack(jnp.maximum(asked[kind], 0), held)
        tiles = [far_move(packed[d], d, 1) for d in range(DESTS)]
        out, d_query, grads = attention(chunk, slots[kind], tile_count, queries, d_attended, tiles)
        product = dot(out, out_grad, 0, 0).astype(jnp.bfloat16)
        partials.append(
            lax.psum_scatter(
                product,
                "seq",
                scatter_dimension=0,
                axis_index_groups=ROWS,
                tiled=True,
            )
        )
        attended.append(out)
        d_queries.append(d_query)
        parts = [far_move(grads[d], d, -1) for d in range(DESTS)]
        sums = merge(asked[kind], parts)
        returned = [near_move(sums[k], -k) for k in range(4)]
        total = sum(r.astype(jnp.float32) for r in returned)
        d_kv.append(total.astype(jnp.bfloat16))
    attended = jnp.concatenate(attended, axis=1)
    joined = jnp.dot(attended, out_weight, preferred_element_type=jnp.float32).astype(jnp.bfloat16)
    partials = jnp.stack(partials)
    arrived = [
        move(lax.dynamic_index_in_dim(partials, (y - k) % NY, 0, keepdims=False), -k, 0, 0)
        for k in range(NY)
    ]
    d_out_weight = sum(part.astype(jnp.float32) for part in arrived)
    d_queries = jnp.concatenate(d_queries, axis=1)
    d_kv = jnp.concatenate(d_kv, axis=3).reshape(rgb_kv.shape)
    return (joined, d_queries, d_kv, d_out_weight)


def solution(mesh):
    placed = (
        P(("clip", "seq"), None),
        P("clip", "seq", None),
        P(("clip", "seq"), None),
        P(("clip", "seq")),
        P(),
        P(("clip", "seq"), None),
    )

    return jax.shard_map(
        local,
        mesh=mesh,
        in_specs=placed,
        out_specs=(
            P(("clip", "seq"), None),
            P(("clip", "seq"), None),
            P("clip", "seq", None),
            P(("clip", "seq"), None),
        ),
        check_vma=False,
    )
```

```python
import functools

import jax
import jax.numpy as jnp
from jax import lax
from jax.experimental import pallas as pl
from jax.experimental.pallas import tpu as pltpu
from jax.sharding import PartitionSpec as P


D = 1024
HEADS = 16
EB = 128
TILE = 128
HEAD_DIM = D // HEADS
SCALE = HEAD_DIM ** -0.5
PAIR = 2 * HEAD_DIM
CHUNKS = 4
COLS = D // CHUNKS
NY, NZ, NCORE = 4, 4, 2
LOCAL = 4
DESTS = 8
masked_score = -1e30


def shift(dy, dz, dc):
    pairs = []
    for y in range(NY):
        for z in range(NZ):
            for c in range(NCORE):
                to = (((y + dy) % NY) * NZ + (z + dz) % NZ) * NCORE + (c ^ dc)
                pairs.append(((y * NZ + z) * NCORE + c, to))
    return pairs


def move(x, dy, dz, dc):
    if dy % NY == 0 and dz % NZ == 0 and dc == 0:
        return x
    return lax.ppermute(x, "seq", shift(dy, dz, dc))


def dot(a, b, ca, cb):
    return lax.dot_general(a, b, (((ca,), (cb,)), ((), ())), preferred_element_type=jnp.float32)


def pack_kernel(index_ref, *refs):
    held, packed, sem = refs[:4], refs[4:12], refs[12]
    copies = []
    for d in range(DESTS):
        for k in range(4):
            copy = pltpu.make_async_copy(
                held[k].at[:, index_ref[d, k]], packed[d].at[:, k], sem.at[d, k]
            )
            copy.start()
            copies.append(copy)
    for copy in copies:
        copy.wait()


def pack(index, held):
    shape = jax.ShapeDtypeStruct((2, 4, TILE, COLS), jnp.bfloat16)
    return pl.pallas_call(
        pack_kernel,
        grid_spec=pltpu.PrefetchScalarGridSpec(
            num_scalar_prefetch=1,
            grid=(1,),
            in_specs=[pl.BlockSpec((2, LOCAL, TILE, COLS), lambda i, index: (0, 0, 0, 0))] * 4,
            out_specs=[pl.BlockSpec(memory_space=pl.ANY)] * DESTS,
            scratch_shapes=[pltpu.SemaphoreType.DMA((DESTS, 4))],
        ),
        out_shape=[shape] * DESTS,
        name="pack",
    )(index, *held)


def merge_kernel(index_ref, *refs):
    parts, sums, acc = refs[:8], refs[8:12], refs[12]
    for k in range(4):
        acc[...] = jnp.zeros_like(acc)
        for d in range(DESTS):
            tile = index_ref[d, k]

            @pl.when(tile >= 0)
            def _():
                acc[tile] += parts[d][0, k].astype(jnp.float32)

        sums[k][0] = acc[...].astype(jnp.bfloat16)


def merge(index, parts):
    block = pl.BlockSpec((1, 4, TILE, COLS), lambda i, index: (i, 0, 0, 0))
    shape = jax.ShapeDtypeStruct((2, 4, TILE, COLS), jnp.bfloat16)
    return pl.pallas_call(
        merge_kernel,
        grid_spec=pltpu.PrefetchScalarGridSpec(
            num_scalar_prefetch=1,
            grid=(2,),
            in_specs=[block] * DESTS,
            out_specs=[block] * 4,
            scratch_shapes=[pltpu.VMEM((LOCAL, TILE, COLS), jnp.float32)],
        ),
        out_shape=[shape] * 4,
        name="merge",
    )(index, *parts)


def attention_kernel(blocks, slot_ref, count_ref, q_ref, do_ref, *refs):
    tiles = refs[:8]
    o_ref, dq_ref = refs[8:10]
    grads = refs[10:18]
    keys, values, d_keys, d_values, own_keys, own_values, scores, weights, d_scores = refs[18:]
    entries = slot_ref.shape[1]
    for d in range(DESTS):
        for k in range(4):
            keys[4 * d + k] = tiles[d][0, k]
            values[4 * d + k] = tiles[d][1, k]
    d_keys[...] = jnp.zeros_like(d_keys)
    d_values[...] = jnp.zeros_like(d_values)

    def split(x, axis):
        low = lax.broadcasted_iota(jnp.int32, x.shape, 1 - axis) < HEAD_DIM
        zero = jnp.zeros_like(x)
        return jnp.concatenate([jnp.where(low, x, zero), jnp.where(low, zero, x)], axis=axis)

    def join(x):
        return jnp.concatenate([x[:HEAD_DIM, :EB], x[HEAD_DIM:, EB:]], axis=0)

    def fold(x, op):
        return op(x.reshape(TILE // 8, 8, 2 * EB), axis=0)

    def block_step(b, carry):
        rows = pl.ds(pl.multiple_of(b * EB, EB), EB)
        count = count_ref[b]
        query = q_ref[rows, :] * jnp.bfloat16(SCALE)
        query2 = split(query, 0)
        parts = [slice(j * TILE, (j + 1) * TILE) for j in range(entries)]
        for j in range(entries):
            own_keys[parts[j], :] = keys[slot_ref[b, j]]
            own_values[parts[j], :] = values[slot_ref[b, j]]
        logits = dot(own_keys[...], query2, 1, 1)
        maxima = jnp.full((8, 2 * EB), masked_score, jnp.float32)
        for j in range(entries):
            masked = jnp.where(j < count, logits[parts[j]], masked_score)
            scores[parts[j], :] = masked
            maxima = jnp.maximum(maxima, fold(masked, jnp.max))
        row_max = jnp.max(maxima, axis=0, keepdims=True)
        total = jnp.zeros((8, 2 * EB), jnp.float32)
        for j in range(entries):
            weight = jnp.exp(scores[parts[j], :] - row_max)
            total += fold(weight, jnp.sum)
            weights[parts[j], :] = weight.astype(jnp.bfloat16)
        inverse = 1.0 / jnp.sum(total, axis=0, keepdims=True)
        out = join(dot(own_values[...], weights[...], 0, 0) * inverse)
        d_out = do_ref[rows, :].astype(jnp.float32).T
        product = out * d_out
        delta = jnp.concatenate(
            [
                jnp.sum(product[:HEAD_DIM], axis=0, keepdims=True),
                jnp.sum(product[HEAD_DIM:], axis=0, keepdims=True),
            ],
            axis=1,
        )
        delta = delta * inverse
        o_ref[rows, :] = out.T.astype(jnp.bfloat16)
        low = lax.broadcasted_iota(jnp.int32, (PAIR, EB), 0) < HEAD_DIM
        scaled = d_out * jnp.where(low, inverse[:, :EB], inverse[:, EB:])
        d_out2 = split(scaled.T.astype(jnp.bfloat16), 0)
        d_weights = dot(own_values[...], d_out2, 1, 1)
        for j in range(entries):
            change = (d_weights[parts[j]] - delta).astype(jnp.bfloat16)
            d_scores[parts[j], :] = weights[parts[j], :] * change
        value_terms = dot(weights[...], d_out2, 1, 0)
        key_terms = dot(d_scores[...], query2, 1, 0)
        for j in range(entries):
            d_values[slot_ref[b, j]] += value_terms[parts[j]]
            d_keys[slot_ref[b, j]] += key_terms[parts[j]]
        d_query = join(dot(own_keys[...], d_scores[...], 0, 0))
        dq_ref[rows, :] = (d_query.T * SCALE).astype(jnp.bfloat16)
        return carry

    lax.fori_loop(0, blocks, block_step, 0, unroll=2)
    for d in range(DESTS):
        for k in range(4):
            grads[d][0, k] = d_keys[4 * d + k].astype(jnp.bfloat16)
            grads[d][1, k] = d_values[4 * d + k].astype(jnp.bfloat16)


def attention(chunk, slots, counts, queries, d_attended, tiles):
    tokens = queries.shape[0]
    blocks = tokens // EB
    entries = slots.shape[1]
    pairs = COLS // PAIR
    wide = pl.BlockSpec((tokens, PAIR), lambda p, s, c: (0, chunk * pairs + p))
    own = pl.BlockSpec((tokens, PAIR), lambda p, s, c: (0, p))
    tile = pl.BlockSpec((2, 4, TILE, PAIR), lambda p, s, c: (0, 0, 0, p))
    out = jax.ShapeDtypeStruct((tokens, COLS), jnp.bfloat16)
    grad = jax.ShapeDtypeStruct((2, 4, TILE, COLS), jnp.bfloat16)
    work = DESTS * 4
    results = pl.pallas_call(
        functools.partial(attention_kernel, blocks),
        grid_spec=pltpu.PrefetchScalarGridSpec(
            num_scalar_prefetch=2,
            grid=(pairs,),
            in_specs=[wide, wide] + [tile] * DESTS,
            out_specs=[own, own] + [tile] * DESTS,
            scratch_shapes=[
                pltpu.VMEM((work, TILE, PAIR), jnp.bfloat16),
                pltpu.VMEM((work, TILE, PAIR), jnp.bfloat16),
                pltpu.VMEM((work, TILE, PAIR), jnp.float32),
                pltpu.VMEM((work, TILE, PAIR), jnp.float32),
                pltpu.VMEM((entries * TILE, PAIR), jnp.bfloat16),
                pltpu.VMEM((entries * TILE, PAIR), jnp.bfloat16),
                pltpu.VMEM((entries * TILE, 2 * EB), jnp.float32),
                pltpu.VMEM((entries * TILE, 2 * EB), jnp.bfloat16),
                pltpu.VMEM((entries * TILE, 2 * EB), jnp.bfloat16),
            ],
        ),
        out_shape=[out, out] + [grad] * DESTS,
        cost_estimate=pl.CostEstimate(
            flops=12 * pairs * blocks * entries * TILE * 2 * EB * PAIR,
            transcendentals=pairs * blocks * entries * TILE * 2 * EB,
            bytes_accessed=4 * work * TILE * COLS * 2,
        ),
        compiler_params=pltpu.CompilerParams(vmem_limit_bytes=56 * 1024 * 1024),
        name="attention",
    )(slots, counts, queries, d_attended, *tiles)
    return results[0], results[1], results[2:]


def local(queries, rgb_kv, tile_ids, tile_count, out_weight, out_grad):
    me = lax.axis_index("seq")
    y, z, c = me // (NZ * NCORE), (me // NCORE) % NZ, me % NCORE
    devices = NY * NZ * NCORE
    own_tiles = rgb_kv.reshape(2, LOCAL, TILE, D)
    source = tile_ids // LOCAL
    within = tile_ids % LOCAL
    usable = jnp.arange(tile_ids.shape[1])[None, :] < tile_count[:, None]
    matches = (source[:, :, None] == jnp.arange(devices)[None, None, :]) & usable[:, :, None]
    wanted = jnp.max(jnp.where(matches, within[:, :, None], -1), axis=(0, 1))
    grid = wanted.reshape(NY, NZ, NCORE)
    along = jnp.concatenate(
        [
            jnp.broadcast_to(grid.transpose(1, 2, 0)[None], (NY, NZ, NCORE, NY)),
            jnp.broadcast_to(grid.transpose(0, 2, 1)[:, None], (NY, NZ, NCORE, NZ)),
        ],
        axis=3,
    )
    told = lax.all_to_all(along.reshape(devices, NY + NZ), "seq", 0, 0, tiled=True)
    told = told.reshape(NY, NZ, NCORE, NY + NZ)
    source_y, source_z = source // (NZ * NCORE), (source // NCORE) % NZ
    flip = (source % NCORE) ^ c
    back_y, back_z = (y - source_y) % NY, (z - source_z) % NZ
    slots = (
        (back_z * NCORE + flip) * 4 + back_y,
        (back_y * NCORE + flip) * 4 + back_z,
    )
    far = jnp.arange(4)[:, None, None]
    core = c ^ jnp.arange(NCORE)[None, :, None]
    near = jnp.arange(4)[None, None, :]
    asked = (
        told[y, (z + far) % NZ, core, (y - near) % NY].reshape(DESTS, 4),
        told[(y + far) % NY, z, core, NY + (z - near) % NZ].reshape(DESTS, 4),
    )

    d_attended = lax.dot_general(
        out_grad, out_weight, (((1,), (1,)), ((), ())), preferred_element_type=jnp.float32
    ).astype(jnp.bfloat16)

    attended, d_queries, d_kv, partials = [], [], [], []
    for chunk in range(CHUNKS):
        along_y = chunk % 2 == 0
        kind = 0 if along_y else 1

        def near_move(x, k):
            return move(x, k, 0, 0) if along_y else move(x, 0, k, 0)

        def far_move(x, d, sign):
            step, core = sign * (d // NCORE), d % NCORE
            return move(x, 0, step, core) if along_y else move(x, step, 0, core)

        mine = own_tiles[..., chunk * COLS : (chunk + 1) * COLS]
        if chunk == 2:
            mine, told = lax.optimization_barrier((mine, told))
        held = [near_move(mine, k) for k in range(4)]
        packed = pack(jnp.maximum(asked[kind], 0), held)
        tiles = [far_move(packed[d], d, 1) for d in range(DESTS)]
        out, d_query, grads = attention(chunk, slots[kind], tile_count, queries, d_attended, tiles)
        partials.append(
            dot(out, out_grad, 0, 0)
            .astype(jnp.bfloat16)
            .reshape(NZ, NCORE, COLS // DESTS, D)
        )
        attended.append(out)
        d_queries.append(d_query)
        parts = [far_move(grads[d], d, -1) for d in range(DESTS)]
        sums = merge(asked[kind], parts)
        returned = [near_move(sums[k], -k) for k in range(4)]
        total = sum(r.astype(jnp.float32) for r in returned)
        d_kv.append(total.astype(jnp.bfloat16))
    attended = jnp.concatenate(attended, axis=1)
    joined = jnp.dot(attended, out_weight, preferred_element_type=jnp.float32).astype(jnp.bfloat16)
    partials = jnp.stack(partials)
    across = []
    for d in range(DESTS):
        to_z, to_core = (z + d // NCORE) % NZ, c ^ (d % NCORE)
        piece = lax.dynamic_slice(
            partials, (0, to_z, to_core, 0, 0), (NY, 1, 1) + partials.shape[3:]
        ).reshape((NY,) + partials.shape[3:])
        across.append(move(piece, 0, d // NCORE, d % NCORE))
    row = sum(part.astype(jnp.float32) for part in across).astype(jnp.bfloat16)
    arrived = [
        move(lax.dynamic_index_in_dim(row, (y - k) % NY, 0, keepdims=False), -k, 0, 0)
        for k in range(NY)
    ]
    d_out_weight = sum(part.astype(jnp.float32) for part in arrived)
    d_queries = jnp.concatenate(d_queries, axis=1)
    d_kv = jnp.concatenate(d_kv, axis=3).reshape(rgb_kv.shape)
    return (joined, d_queries, d_kv, d_out_weight)


def solution(mesh):
    placed = (
        P(("clip", "seq"), None),
        P("clip", "seq", None),
        P(("clip", "seq"), None),
        P(("clip", "seq")),
        P(),
        P(("clip", "seq"), None),
    )

    return jax.shard_map(
        local,
        mesh=mesh,
        in_specs=placed,
        out_specs=(
            P(("clip", "seq"), None),
            P(("clip", "seq"), None),
            P("clip", "seq", None),
            P(("clip", "seq"), None),
        ),
        check_vma=False,
    )
```
